256 devices in a mesh: mom: 64 (over z, x, core), tm: 4 (over y).
Axes of the slice: x: 4, y: 4, z: 8, core: 2. Of those that a mesh axis runs over, the one named last changes fastest.
Arguments:
- new_rows: float32 [4, 256, 16, 512], P(None, 'mom', None, 'tm'), may hold values from -9 to 9
- history: float32 [3, 2, 256, 512, 512], P(None, None, 'mom', 'tm'), may hold values from -0.25 to 0.25
- momentum_map: int32 [256], replicated, may hold values from 0 to 255, each once
- step_index: int32 [1], replicated, may hold values from 0 to 999
- history_len: int32 [1], replicated, may hold values from 256 to 512
Outputs:
- advanced_rows: float32 [4, 256, 16, 512], P(None, 'mom', None, 'tm')
The draws below stay inside these ranges and needn't reach their ends.
Inputs may be any that keep to these rules, and one draw needn't show every extreme that they name: `momentum_map`: each number of 0 to 255 appears once.
All inputs are finite; a program needn't handle non-finite values.
Results may differ from the reference program's by a relative error of at most 0.0003.
Values sent between devices are 32-bit elements; how exact they have to be, the bound alone decides.
No kernel may reach another device: no remote copies, remote signals or barrier semaphores. Data moves between devices by JAX's collectives and lax.ppermute only.
A program may use at most 128 MiB of HBM per device.

```python
import jax
import jax.numpy as jnp
from jax import lax

SIDE = 16
MOMENTA = 256
HIST = 512
ROWS = 16


def levels(rng, extent, pieces, low, largest):
    loudness, own = 1.0, jax.random.fold_in(rng, 6)
    for dim, shards_of in pieces:
        steps = jnp.exp(jax.random.uniform(jax.random.fold_in(own, dim), (shards_of,), jnp.float32, low / len(pieces), largest / len(pieces)))
        loudness = loudness * jnp.repeat(steps, extent[dim] // shards_of).reshape([-1 if axis == dim else 1 for axis in range(len(extent))])
    return loudness


def noise(rng, shape, spread, reach, split=(), kind=jnp.bfloat16):
    factor_of = levels(rng, shape, split, -0.22, 0.18) if split else 1.0
    array = jax.random.normal(rng, shape, jnp.float32) * spread * factor_of
    return jnp.minimum(jnp.maximum(array, -reach), reach).astype(kind)


def setup_inputs(seed: int = 0) -> dict:
    splits = jax.random.split(jax.random.key(seed), 6)
    return {
        "new_rows": noise(splits[0], (4, MOMENTA, ROWS, HIST), 1.5, 9.0, ((1, 64), (3, 4)), jnp.float32),
        "history": noise(splits[1], (3, 2, MOMENTA, HIST, HIST), HIST ** -0.5, 0.25, ((2, 64), (3, 4)), jnp.float32),
        "momentum_map": jax.random.permutation(splits[2], MOMENTA).astype(jnp.int32),
        "step_index": jax.random.randint(splits[3], (1,), 0, 1000).astype(jnp.int32),
        "history_len": jax.random.randint(splits[4], (1,), HIST // 2, HIST + 1).astype(jnp.int32),
    }


TIME_STEP = 0.2
COUPLING = 5.0
DRIVE_RATE = 0.3
PRECISE = lax.Precision.HIGHEST


def lattice_tables(momentum_map, side):
    mom_count = momentum_map.shape[0]
    sites = jnp.arange(mom_count, dtype=jnp.int32)
    mom_x = momentum_map // side
    mom_y = momentum_map % side
    site_x = sites // side
    site_y = sites % side
    winding = (site_x[:, None] * mom_x[None, :] + site_y[:, None] * mom_y[None, :]) % side
    phases = winding.astype(jnp.float32) * (2.0 * jnp.pi / side)
    return jnp.cos(phases), jnp.sin(phases)


def band_energy(own_map, row_times, side):
    wave_x = (own_map // side).astype(jnp.float32) * (2.0 * jnp.pi / side)
    wave_y = (own_map % side).astype(jnp.float32) * (2.0 * jnp.pi / side)
    drift = DRIVE_RATE * row_times
    return -2.0 * (jnp.cos(wave_x[:, None] + drift[None, :]) + jnp.cos(wave_y[:, None] + drift[None, :]))


def to_sites(cosine_table, sine_table, lattice):
    mom_count = lattice.shape[1]
    paired = lattice.reshape(2, 2, mom_count, lattice.shape[2])
    parts_re = paired[:, 0]
    parts_im = paired[:, 1]

    def apply_table(table, values):
        return jnp.einsum("rk,wkc->wrc", table, values, precision=PRECISE)

    site_re = (apply_table(cosine_table, parts_re) - apply_table(sine_table, parts_im)) / mom_count
    site_im = (apply_table(cosine_table, parts_im) + apply_table(sine_table, parts_re)) / mom_count
    return jnp.stack([site_re, site_im], axis=1).reshape(4, cosine_table.shape[0], lattice.shape[2])


def from_sites(cosine_table, sine_table, lattice):
    paired = lattice.reshape(2, 2, lattice.shape[1], lattice.shape[2])
    parts_re = paired[:, 0]
    parts_im = paired[:, 1]

    def apply_table(table, values):
        return jnp.einsum("rk,wrc->wkc", table, values, precision=PRECISE)

    mom_re = apply_table(cosine_table, parts_re) + apply_table(sine_table, parts_im)
    mom_im = apply_table(cosine_table, parts_im) - apply_table(sine_table, parts_re)
    return jnp.stack([mom_re, mom_im], axis=1).reshape(4, cosine_table.shape[1], lattice.shape[2])


def bubble_term(left_re, left_im, right_re, right_im):
    square_re = left_re * left_re - left_im * left_im
    square_im = 2.0 * left_re * left_im
    factor = -COUPLING * COUPLING
    return factor * (square_re * right_re + square_im * right_im), factor * (square_im * right_re - square_re * right_im)


def bubble(lattice):
    ret_re, ret_im, less_re, less_im = lattice[0], lattice[1], lattice[2], lattice[3]
    great_re = less_re + ret_re
    great_im = less_im + ret_im
    lesser_re, lesser_im = bubble_term(less_re, less_im, great_re, great_im)
    greater_re, greater_im = bubble_term(great_re, great_im, less_re, less_im)
    return jnp.stack([greater_re - lesser_re, greater_im - lesser_im, lesser_re, lesser_im])


def contract(energy_pair, stored_pair):
    product = jnp.einsum("akiu,bkus->abkis", energy_pair, stored_pair, precision=PRECISE)
    return product[0, 0] - product[1, 1], product[0, 1] + product[1, 0]


def memory_integral(self_energy, history):
    ret_ret = contract(self_energy[0:2], history[0])
    ret_less = contract(self_energy[0:2], history[1])
    less_adv = contract(self_energy[2:4], history[2])
    return TIME_STEP * jnp.stack([ret_ret[0], ret_ret[1], ret_less[0] + less_adv[0], ret_less[1] + less_adv[1]])


def rotate(total):
    return jnp.stack([total[1], -total[0], total[3], -total[2]])


def reference(new_rows, history, momentum_map, step_index, history_len):
    mom_count = new_rows.shape[1]
    row_count = new_rows.shape[2]
    time_count = new_rows.shape[3]
    cosine_table, sine_table = lattice_tables(momentum_map, SIDE)
    memory_mask = (jnp.arange(time_count, dtype=jnp.int32) < history_len[0]).astype(jnp.float32)
    first_times = step_index[0].astype(jnp.float32) + jnp.arange(row_count, dtype=jnp.int32).astype(jnp.float32)

    def slope(estimate, offset_steps):
        band = band_energy(momentum_map, (first_times + offset_steps) * TIME_STEP, SIDE)
        lattice = to_sites(cosine_table, sine_table, estimate.reshape(4, mom_count, row_count * time_count))
        self_energy = from_sites(cosine_table, sine_table, bubble(lattice))
        self_energy = self_energy.reshape(4, mom_count, row_count, time_count) * memory_mask
        integral = memory_integral(self_energy, history)
        return rotate(band[None, :, :, None] * estimate + integral)

    current = new_rows
    for time_step in range(2):
        slope_now = slope(current, float(time_step))
        estimate = current + TIME_STEP * slope_now
        for corrector in range(2):
            estimate = current + 0.5 * TIME_STEP * (slope_now + slope(estimate, float(time_step + 1)))
        current = estimate
    return current
```

```python
import functools

import jax
import jax.numpy as jnp
from jax import lax
from jax.experimental import pallas as pl
from jax.experimental.pallas import tpu as pltpu
from jax.sharding import PartitionSpec as P

SIDE = 16
TIME_STEP = 0.2
COUPLING = 5.0
DRIVE_RATE = 0.3
LANES = 128
GROUP = 32
F32 = jnp.float32
BF16 = jnp.bfloat16


def lane_group(shape):
    return lax.broadcasted_iota(jnp.int32, shape, len(shape) - 1) // GROUP


def swap_groups(blocks):
    group = lane_group(blocks[0].shape)
    outs = []
    for c in range(4):
        out = None
        for q in range(4):
            shift = (GROUP * (q - c)) % LANES
            piece = pltpu.roll(blocks[q], shift, 1) if shift else blocks[q]
            out = piece if out is None else jnp.where(group == q, piece, out)
        outs.append(out)
    return outs


def split_high_low(value):
    high = value.astype(BF16)
    low = (value - high.astype(F32)).astype(BF16)
    return high, low


def times_minus_i(value):
    even = lane_group(value.shape) % 2 == 0
    return jnp.where(even, pltpu.roll(value, LANES - GROUP, 1), -pltpu.roll(value, GROUP, 1))


def resident(kernel, out_shapes, in_spaces, name, scratch=(), limit=4 << 20):
    results = [pltpu.VMEM(o.shape, o.dtype) for o in out_shapes]
    call = pl.pallas_call(
        kernel,
        in_specs=[pl.BlockSpec(memory_space=space) for space in in_spaces],
        out_specs=[pl.BlockSpec(memory_space=pltpu.VMEM)] * len(results),
        out_shape=results,
        scratch_shapes=scratch,
        compiler_params=pltpu.CompilerParams(vmem_limit_bytes=limit),
        name=name,
    )

    def apply(*values):
        placed = [
            value if space is pltpu.SMEM else pltpu.with_memory_space_constraint(value, space)
            for value, space in zip(values, in_spaces, strict=True)
        ]
        return call(*placed)

    return apply


def pack_kernel(rows_ref, out_ref):
    row_count = rows_ref.shape[2]
    own = rows_ref.shape[1]
    for k in range(own):
        packed = swap_groups([rows_ref[c, k] for c in range(4)])
        for q in range(4):
            out_ref[pl.ds(q * own * row_count + k, row_count, stride=own), :] = packed[q]


def history_kernel(stored_ref, high_ref, low_ref, buffer_ref, arrived):
    kinds, parts, own, times, _ = stored_ref.shape
    slots = buffer_ref.shape[0]

    def fetch(n):
        slot = n % slots
        return pltpu.make_async_copy(stored_ref.at[n // parts, n % parts], buffer_ref.at[slot], arrived.at[slot])

    for n in range(slots):
        fetch(n).start()
    for n in range(kinds * parts):
        fetch(n).wait()
        for k in range(own):
            high, low = split_high_low(buffer_ref[n % slots, k])
            high_ref[k, n * times : (n + 1) * times, :] = high
            low_ref[k, n * times : (n + 1) * times, :] = low
        if n + slots < kinds * parts:
            fetch(n + slots).start()


def transform(table_ref, value, turned):
    value_high, value_low = split_high_low(value)
    turned_high, turned_low = split_high_low(turned)
    operand = jnp.concatenate(
        [
            jnp.concatenate([value_high, value_low], axis=1),
            jnp.concatenate([turned_high, turned_low], axis=1),
        ],
        axis=0,
    )
    depth = operand.shape[0]
    total = jnp.dot(table_ref[:, :depth], operand, preferred_element_type=F32)
    total = total + jnp.dot(table_ref[:, depth:], operand, preferred_element_type=F32)
    return total[:, :LANES] + total[:, LANES:]


def site_kernel(table_ref, rows_ref, out_ref):
    mom_count = rows_ref.shape[0]
    rows = rows_ref[...]
    group = lane_group(rows.shape)
    even = group % 2 == 0
    upper = group >= 2
    sites = transform(table_ref, rows, -times_minus_i(rows)) * (1.0 / mom_count)
    other = pltpu.roll(sites, 2 * GROUP, 1)
    great = sites + other
    less = jnp.where(upper, sites, other)
    great_turn = pltpu.roll(great, GROUP, 1)
    less_turn = pltpu.roll(less, GROUP, 1)
    pair = jnp.where(even, less * great + less_turn * great_turn, less * great_turn - less_turn * great)
    pair_turn = pltpu.roll(pair, GROUP, 1)
    lesser = jnp.where(even, less * pair - less_turn * pair_turn, less * pair_turn + less_turn * pair)
    greater = jnp.where(even, great * pair + great_turn * pair_turn, great * pair_turn - great_turn * pair)
    energy = (-COUPLING * COUPLING) * jnp.where(upper, lesser, greater - lesser)
    out_ref[...] = transform(table_ref, energy, times_minus_i(energy))


def integral_kernel(limits_ref, energy_ref, high_ref, low_ref, out_ref, split_ref):
    own = high_ref.shape[0]
    block = split_ref.shape[1]
    rows = block // own
    position = limits_ref[0] + lax.broadcasted_iota(jnp.int32, (block, LANES), 1)
    mask = (position < limits_ref[1]).astype(F32)
    parts = swap_groups([energy_ref[q * block : (q + 1) * block, :] for q in range(4)])
    for c in range(4):
        split_ref[c] = parts[c] * mask

    def left(k, pair):
        real = split_ref[2 * pair, pl.ds(k, rows, stride=own), :]
        imag = split_ref[2 * pair + 1, pl.ds(k, rows, stride=own), :]
        joined = jnp.concatenate(
            [jnp.concatenate([real, -imag], axis=1), jnp.concatenate([imag, real], axis=1)], axis=0
        )
        high, low = split_high_low(joined)
        return jnp.concatenate([high, low], axis=0)

    for k in range(own):
        retarded_left = left(k, 0)
        lesser_left = jnp.concatenate([retarded_left, left(k, 1)], axis=1)

        def product(lhs, start, stop):
            both = jnp.dot(lhs, high_ref[k, start:stop, :], preferred_element_type=F32)
            small = jnp.dot(lhs[: 2 * rows], low_ref[k, start:stop, :], preferred_element_type=F32)
            return TIME_STEP * (both[: 2 * rows] + both[2 * rows :] + small)

        retarded = product(retarded_left, 0, 2 * LANES)
        lesser = product(lesser_left, 2 * LANES, 6 * LANES)
        values = (retarded[:rows], retarded[rows:], lesser[:rows], lesser[rows:])
        for t in range(out_ref.shape[0]):
            for c, value in enumerate(values):
                out_ref[t, pl.ds(c * block + k, rows, stride=own), :] = value[:, t * LANES : (t + 1) * LANES]


def slope_of(parts_ref, state, band_ref):
    block = band_ref.shape[0]
    total = parts_ref[0]
    for t in range(1, parts_ref.shape[0]):
        total = total + parts_ref[t]
    packed = swap_groups([total[c * block : (c + 1) * block] for c in range(4)])
    band = band_ref[...]
    return jnp.concatenate(
        [times_minus_i(band * state[q * block : (q + 1) * block] + packed[q]) for q in range(4)], axis=0
    )


def predict_kernel(parts_ref, state_ref, band_ref, out_ref, base_ref):
    state = state_ref[...]
    slope = slope_of(parts_ref, state, band_ref)
    out_ref[...] = state + TIME_STEP * slope
    base_ref[...] = state + (0.5 * TIME_STEP) * slope


def correct_kernel(parts_ref, state_ref, band_ref, base_ref, out_ref):
    slope = slope_of(parts_ref, state_ref[...], band_ref)
    out_ref[...] = base_ref[...] + (0.5 * TIME_STEP) * slope


def last_kernel(parts_ref, state_ref, band_ref, base_ref, out_ref, split_ref):
    slope = slope_of(parts_ref, state_ref[...], band_ref)
    value = base_ref[...] + (0.5 * TIME_STEP) * slope
    block = band_ref.shape[0]
    parts = swap_groups([value[q * block : (q + 1) * block] for q in range(4)])
    own, rows = out_ref.shape[1], out_ref.shape[2]
    for c in range(4):
        split_ref[c] = parts[c]
        for k in range(own):
            out_ref[c, k] = split_ref[c, pl.ds(k, rows, stride=own), :]


def transform_tables(momentum_map):
    point_x = momentum_map // SIDE
    point_y = momentum_map % SIDE
    winding = (point_x[:, None] * point_x[None, :] + point_y[:, None] * point_y[None, :]) % SIDE
    phases = winding.astype(F32) * (2.0 * jnp.pi / SIDE)
    parts = []
    for table in (jnp.cos(phases), jnp.sin(phases)):
        high = lax.reduce_precision(table, 8, 7)
        parts.append((high.astype(BF16), (table - high).astype(BF16)))
    (cos_high, cos_low), (sin_high, sin_low) = parts
    return jnp.concatenate([cos_high, sin_high, cos_low, sin_low], axis=1)


def band_rows(own_map, first_times, offset):
    wave_x = (own_map // SIDE).astype(F32) * (2.0 * jnp.pi / SIDE)
    wave_y = (own_map % SIDE).astype(F32) * (2.0 * jnp.pi / SIDE)
    drift = DRIVE_RATE * ((first_times + offset) * TIME_STEP)
    band = -2.0 * (jnp.cos(wave_x[None, :] + drift[:, None]) + jnp.cos(wave_y[None, :] + drift[:, None]))
    return jnp.broadcast_to(band.reshape(-1, 1), (band.size, LANES))


def body(new_rows, history, momentum_map, step_index, history_len):
    own = new_rows.shape[1]
    row_count = new_rows.shape[2]
    time_count = new_rows.shape[3]
    hist = history.shape[4]
    block = own * row_count
    packed_shape = jax.ShapeDtypeStruct((4 * block, time_count), F32)

    table = transform_tables(momentum_map)
    own_map = lax.dynamic_slice_in_dim(momentum_map, lax.axis_index("mom") * own, own, 0)
    first_times = step_index[0].astype(F32) + jnp.arange(row_count, dtype=jnp.int32).astype(F32)
    bands = [band_rows(own_map, first_times, float(offset)) for offset in range(3)]
    limits = jnp.stack([lax.axis_index("tm") * time_count, history_len[0]])

    vmem = pltpu.VMEM
    pack = resident(pack_kernel, [packed_shape], [vmem], "pack")
    stored = 6 * time_count
    split_shape = jax.ShapeDtypeStruct((own, stored, hist), BF16)
    split_history = resident(
        history_kernel,
        [split_shape] * 2,
        [pltpu.HBM],
        "split_history",
        [vmem((3, *history.shape[2:]), F32), pltpu.SemaphoreType.DMA((3,))],
        5 << 20,
    )
    site = resident(site_kernel, [packed_shape], [vmem] * 2, "site")
    tm_size = lax.axis_size("tm")
    parts_shape = jax.ShapeDtypeStruct((tm_size, 4 * block, LANES), F32)
    integral = resident(
        integral_kernel, [parts_shape], [pltpu.SMEM] + [vmem] * 3, "integral", [vmem((4, block, LANES), F32)]
    )
    predict = resident(predict_kernel, [packed_shape] * 2, [vmem] * 3, "predict")
    correct = resident(correct_kernel, [packed_shape], [vmem] * 4, "correct")
    last = pl.pallas_call(
        last_kernel,
        out_shape=jax.ShapeDtypeStruct(new_rows.shape, F32),
        scratch_shapes=[pltpu.VMEM((4, block, LANES), F32)],
        name="last",
    )

    (state,) = pack(new_rows)
    high, low = split_history(history)

    def turned(value):
        return lax.all_to_all(value, "mom", 0, 0, tiled=True)

    def parts_of(arrived):
        (energy,) = site(table, arrived)
        (partial,) = integral(limits, turned(energy), high, low)
        return lax.all_to_all(partial, "tm", 0, 0, tiled=True)

    first = turned(state)
    first, table, high, low, limits, bands, state = lax.optimization_barrier(
        (first, table, high, low, limits, bands, state)
    )

    for time_step in range(2):
        arrived = first if time_step == 0 else turned(state)
        estimate, base = predict(parts_of(arrived), state, bands[time_step])
        (estimate,) = correct(parts_of(turned(estimate)), estimate, bands[time_step + 1], base)
        if time_step == 0:
            (state,) = correct(parts_of(turned(estimate)), estimate, bands[time_step + 1], base)
    return last(parts_of(turned(estimate)), estimate, bands[2], base)


def solution(mesh):
    return jax.shard_map(
        body,
        mesh=mesh,
        in_specs=(P(None, "mom", None, "tm"), P(None, None, "mom", "tm", None), P(), P(), P()),
        out_specs=P(None, "mom", None, "tm"),
        check_vma=False,
    )
```

```python
import functools

import jax
import jax.numpy as jnp
from jax import lax
from jax.experimental import pallas as pl
from jax.experimental.pallas import tpu as pltpu
from jax.sharding import PartitionSpec as P

SIDE = 16
TIME_STEP = 0.2
COUPLING = 5.0
DRIVE_RATE = 0.3
LANES = 128
GROUP = 32
F32 = jnp.float32
BF16 = jnp.bfloat16


def lane_group(shape):
    return lax.broadcasted_iota(jnp.int32, shape, len(shape) - 1) // GROUP


def swap_groups(blocks):
    group = lane_group(blocks[0].shape)
    outs = []
    for c in range(4):
        out = None
        for q in range(4):
            shift = (GROUP * (q - c)) % LANES
            piece = pltpu.roll(blocks[q], shift, 1) if shift else blocks[q]
            out = piece if out is None else jnp.where(group == q, piece, out)
        outs.append(out)
    return outs


def split_high_low(value):
    high = value.astype(BF16)
    low = (value - high.astype(F32)).astype(BF16)
    return high, low


def times_minus_i(value):
    even = lane_group(value.shape) % 2 == 0
    return jnp.where(even, pltpu.roll(value, LANES - GROUP, 1), -pltpu.roll(value, GROUP, 1))


def resident(kernel, out_shapes, in_spaces, name, scratch=(), limit=4 << 20):
    results = [pltpu.VMEM(o.shape, o.dtype) for o in out_shapes]
    call = pl.pallas_call(
        kernel,
        in_specs=[pl.BlockSpec(memory_space=space) for space in in_spaces],
        out_specs=[pl.BlockSpec(memory_space=pltpu.VMEM)] * len(results),
        out_shape=results,
        scratch_shapes=scratch,
        compiler_params=pltpu.CompilerParams(vmem_limit_bytes=limit),
        name=name,
    )

    def apply(*values):
        placed = [
            value if space is pltpu.SMEM else pltpu.with_memory_space_constraint(value, space)
            for value, space in zip(values, in_spaces, strict=True)
        ]
        return call(*placed)

    return apply


def pack_kernel(rows_ref, out_ref):
    row_count = rows_ref.shape[2]
    own = rows_ref.shape[1]
    for k in range(own):
        packed = swap_groups([rows_ref[c, k] for c in range(4)])
        for q in range(4):
            out_ref[pl.ds(q * own * row_count + k, row_count, stride=own), :] = packed[q]


def transform(table_ref, value, turned):
    value_high, value_low = split_high_low(value)
    turned_high, turned_low = split_high_low(turned)
    operand = jnp.concatenate(
        [
            jnp.concatenate([value_high, value_low], axis=1),
            jnp.concatenate([turned_high, turned_low], axis=1),
        ],
        axis=0,
    )
    depth = operand.shape[0]
    total = jnp.dot(table_ref[:, :depth], operand, preferred_element_type=F32)
    total = total + jnp.dot(table_ref[:, depth:], operand, preferred_element_type=F32)
    return total[:, :LANES] + total[:, LANES:]


def site_kernel(table_ref, rows_ref, out_ref):
    mom_count = rows_ref.shape[0]
    rows = rows_ref[...]
    group = lane_group(rows.shape)
    even = group % 2 == 0
    upper = group >= 2
    sites = transform(table_ref, rows, -times_minus_i(rows)) * (1.0 / mom_count)
    other = pltpu.roll(sites, 2 * GROUP, 1)
    great = sites + other
    less = jnp.where(upper, sites, other)
    great_turn = pltpu.roll(great, GROUP, 1)
    less_turn = pltpu.roll(less, GROUP, 1)
    pair = jnp.where(even, less * great + less_turn * great_turn, less * great_turn - less_turn * great)
    pair_turn = pltpu.roll(pair, GROUP, 1)
    lesser = jnp.where(even, less * pair - less_turn * pair_turn, less * pair_turn + less_turn * pair)
    greater = jnp.where(even, great * pair + great_turn * pair_turn, great * pair_turn - great_turn * pair)
    energy = (-COUPLING * COUPLING) * jnp.where(upper, lesser, greater - lesser)
    out_ref[...] = transform(table_ref, energy, times_minus_i(energy))


def integral_into(limits_ref, energy_ref, parts_ref, out_refs, split_ref, prepare=None):
    step_one = limits_ref[0] % 2 == 1
    step_two = limits_ref[0] // 2 == 1
    own = parts_ref.shape[1]
    block = split_ref.shape[1]
    rows = block // own
    position = limits_ref[0] * LANES + lax.broadcasted_iota(jnp.int32, (block, LANES), 1)
    mask = (position < limits_ref[1]).astype(F32)
    parts = swap_groups([energy_ref[q * block : (q + 1) * block, :] for q in range(4)])
    for c in range(4):
        split_ref[c] = parts[c] * mask

    def left(k, pair):
        real = split_ref[2 * pair, pl.ds(k, rows, stride=own), :]
        imag = split_ref[2 * pair + 1, pl.ds(k, rows, stride=own), :]
        joined = jnp.concatenate(
            [jnp.concatenate([real, -imag], axis=1), jnp.concatenate([imag, real], axis=1)], axis=0
        )
        high, low = split_high_low(joined)
        return jnp.concatenate([high, low], axis=0)

    def product(k, lhs, start, stop):
        both = jnp.dot(lhs, parts_ref[0, k, start:stop, :], preferred_element_type=F32)
        small = jnp.dot(lhs[: 2 * rows], parts_ref[1, k, start:stop, :], preferred_element_type=F32)
        return TIME_STEP * (both[: 2 * rows] + both[2 * rows :] + small)

    def each(k, carry):
        if prepare is not None:
            prepare(k)
        retarded_left = left(k, 0)
        lesser_left = jnp.concatenate([retarded_left, left(k, 1)], axis=1)
        retarded = product(k, retarded_left, 0, 2 * LANES)
        lesser = product(k, lesser_left, 2 * LANES, 6 * LANES)
        values = (retarded[:rows], retarded[rows:], lesser[:rows], lesser[rows:])
        for c, value in enumerate(values):
            pieces = [value[:, t * LANES : (t + 1) * LANES] for t in range(4)]
            pieces = [jnp.where(step_one, pieces[(t + 1) % 4], pieces[t]) for t in range(4)]
            pieces = [jnp.where(step_two, pieces[(t + 2) % 4], pieces[t]) for t in range(4)]
            for piece, out_ref in zip(pieces, out_refs, strict=True):
                out_ref[pl.ds(c * block + k, rows, stride=own), :] = piece
        return carry

    lax.fori_loop(0, own // 2, lambda pair, carry: each(2 * pair + 1, each(2 * pair, carry)), 0)


def integral_kernel(limits_ref, energy_ref, parts_ref, *refs):
    *out_refs, split_ref = refs
    integral_into(limits_ref, energy_ref, parts_ref, out_refs, split_ref)


def first_integral_kernel(limits_ref, energy_ref, stored_ref, *refs):
    *out_refs, parts_ref, split_ref, buffer_ref, arrived = refs
    kinds, halves, own, times, _ = stored_ref.shape

    def fetch(k, n):
        source = stored_ref.at[n // halves, n % halves, k]
        return pltpu.make_async_copy(source, buffer_ref.at[k, n], arrived.at[k, n])

    for k in range(own):
        for n in range(kinds * halves):
            fetch(k, n).start()

    def prepare(k):
        for n in range(kinds * halves):
            fetch(k, n).wait()
            high, low = split_high_low(buffer_ref[k, n])
            parts_ref[0, k, n * times : (n + 1) * times, :] = high
            parts_ref[1, k, n * times : (n + 1) * times, :] = low

    integral_into(limits_ref, energy_ref, parts_ref, out_refs, split_ref, prepare)


def slope_of(parts, state, band_ref):
    block = band_ref.shape[0]
    total = (parts[0][...] + parts[1][...]) + (parts[2][...] + parts[3][...])
    packed = swap_groups([total[c * block : (c + 1) * block] for c in range(4)])
    band = band_ref[...]
    return jnp.concatenate(
        [times_minus_i(band * state[q * block : (q + 1) * block] + packed[q]) for q in range(4)], axis=0
    )


def predict_kernel(own_ref, one_ref, two_ref, three_ref, state_ref, band_ref, out_ref, base_ref):
    state = state_ref[...]
    slope = slope_of((own_ref, one_ref, two_ref, three_ref), state, band_ref)
    out_ref[...] = state + TIME_STEP * slope
    base_ref[...] = state + (0.5 * TIME_STEP) * slope


def correct_kernel(own_ref, one_ref, two_ref, three_ref, state_ref, band_ref, base_ref, out_ref):
    slope = slope_of((own_ref, one_ref, two_ref, three_ref), state_ref[...], band_ref)
    out_ref[...] = base_ref[...] + (0.5 * TIME_STEP) * slope


def last_kernel(own_ref, one_ref, two_ref, three_ref, state_ref, band_ref, base_ref, out_ref, split_ref):
    slope = slope_of((own_ref, one_ref, two_ref, three_ref), state_ref[...], band_ref)
    value = base_ref[...] + (0.5 * TIME_STEP) * slope
    block = band_ref.shape[0]
    parts = swap_groups([value[q * block : (q + 1) * block] for q in range(4)])
    own, rows = out_ref.shape[1], out_ref.shape[2]
    for c in range(4):
        split_ref[c] = parts[c]
        for k in range(own):
            out_ref[c, k] = split_ref[c, pl.ds(k, rows, stride=own), :]


def transform_tables(momentum_map):
    point_x = momentum_map // SIDE
    point_y = momentum_map % SIDE
    winding = (point_x[:, None] * point_x[None, :] + point_y[:, None] * point_y[None, :]) % SIDE
    phases = winding.astype(F32) * (2.0 * jnp.pi / SIDE)
    parts = []
    for table in (jnp.cos(phases), jnp.sin(phases)):
        high = lax.reduce_precision(table, 8, 7)
        parts.append((high.astype(BF16), (table - high).astype(BF16)))
    (cos_high, cos_low), (sin_high, sin_low) = parts
    return jnp.concatenate([cos_high, sin_high, cos_low, sin_low], axis=1)


def band_rows(own_map, first_times, offset):
    wave_x = (own_map // SIDE).astype(F32) * (2.0 * jnp.pi / SIDE)
    wave_y = (own_map % SIDE).astype(F32) * (2.0 * jnp.pi / SIDE)
    drift = DRIVE_RATE * ((first_times + offset) * TIME_STEP)
    band = -2.0 * (jnp.cos(wave_x[None, :] + drift[:, None]) + jnp.cos(wave_y[None, :] + drift[:, None]))
    return jnp.broadcast_to(band.reshape(-1, 1), (band.size, LANES))


def body(new_rows, history, momentum_map, step_index, history_len):
    own = new_rows.shape[1]
    row_count = new_rows.shape[2]
    time_count = new_rows.shape[3]
    hist = history.shape[4]
    block = own * row_count
    packed_shape = jax.ShapeDtypeStruct((4 * block, time_count), F32)

    table = transform_tables(momentum_map)
    own_map = lax.dynamic_slice_in_dim(momentum_map, lax.axis_index("mom") * own, own, 0)
    first_times = step_index[0].astype(F32) + jnp.arange(row_count, dtype=jnp.int32).astype(F32)
    bands = [band_rows(own_map, first_times, float(offset)) for offset in range(3)]
    limits = jnp.stack([lax.axis_index("tm"), history_len[0]])

    vmem = pltpu.VMEM
    pack = resident(pack_kernel, [packed_shape], [vmem], "pack")
    stored = 6 * time_count
    parts_shape = jax.ShapeDtypeStruct((2, own, stored, hist), BF16)
    site = resident(site_kernel, [packed_shape], [vmem] * 2, "site")
    tm_size = lax.axis_size("tm")
    split_scratch = vmem((4, block, LANES), F32)
    integral = resident(
        integral_kernel, [packed_shape] * tm_size, [pltpu.SMEM, vmem, vmem], "integral", [split_scratch]
    )
    first_integral = resident(
        first_integral_kernel,
        [packed_shape] * tm_size + [parts_shape],
        [pltpu.SMEM, vmem, pltpu.HBM],
        "first_integral",
        [split_scratch, vmem((own, 6, time_count, hist), F32), pltpu.SemaphoreType.DMA((own, 6))],
        9 << 20,
    )
    predict = resident(predict_kernel, [packed_shape] * 2, [vmem] * 6, "predict")
    correct = resident(correct_kernel, [packed_shape], [vmem] * 7, "correct")
    last = resident(
        last_kernel, [jax.ShapeDtypeStruct(new_rows.shape, F32)], [vmem] * 7, "last", [split_scratch]
    )
    (state,) = pack(new_rows)

    def turned(value):
        return lax.all_to_all(value, "mom", 0, 0, tiled=True)

    def exchange(partial):
        hops = {n: [(t, (t + n) % tm_size) for t in range(tm_size)] for n in (2, 1, 3)}
        parts = {n: lax.ppermute(partial[n], "tm", hop) for n, hop in hops.items()}
        return partial[0], parts[2], parts[1], parts[3]

    def energy_of(arrived):
        (energy,) = site(table, arrived)
        return turned(energy)

    first = turned(state)
    first, limits, bands = lax.optimization_barrier((first, limits, bands))
    *partial, stored_parts = first_integral(limits, energy_of(first), history)

    def parts_of(estimate):
        return exchange(integral(limits, energy_of(turned(estimate)), stored_parts))

    for time_step in range(2):
        parts = exchange(partial) if time_step == 0 else parts_of(state)
        estimate, base = predict(*parts, state, bands[time_step])
        (estimate,) = correct(*parts_of(estimate), estimate, bands[time_step + 1], base)
        if time_step == 0:
            (state,) = correct(*parts_of(estimate), estimate, bands[1], base)
    return last(*parts_of(estimate), estimate, bands[2], base)[0]


def solution(mesh):
    return jax.shard_map(
        body,
        mesh=mesh,
        in_specs=(P(None, "mom", None, "tm"), P(None, None, "mom", "tm", None), P(), P(), P()),
        out_specs=P(None, "mom", None, "tm"),
        check_vma=False,
    )
```

```python
import functools

import jax
import jax.numpy as jnp
from jax import lax
from jax.experimental import pallas as pl
from jax.experimental.pallas import tpu as pltpu
from jax.sharding import PartitionSpec as P

SIDE = 16
TIME_STEP = 0.2
COUPLING = 5.0
DRIVE_RATE = 0.3
LANES = 128
GROUP = 32
F32 = jnp.float32
BF16 = jnp.bfloat16


def lane_group(shape):
    return lax.broadcasted_iota(jnp.int32, shape, len(shape) - 1) // GROUP


def swap_groups(blocks):
    group = lane_group(blocks[0].shape)
    outs = []
    for c in range(4):
        out = None
        for q in range(4):
            shift = (GROUP * (q - c)) % LANES
            piece = pltpu.roll(blocks[q], shift, 1) if shift else blocks[q]
            out = piece if out is None else jnp.where(group == q, piece, out)
        outs.append(out)
    return outs


def split_high_low(value):
    high = value.astype(BF16)
    low = (value - high.astype(F32)).astype(BF16)
    return high, low


def times_minus_i(value):
    even = lane_group(value.shape) % 2 == 0
    return jnp.where(even, pltpu.roll(value, LANES - GROUP, 1), -pltpu.roll(value, GROUP, 1))


def resident(kernel, out_shapes, in_spaces, name, scratch=(), limit=4 << 20, cost=None):
    results = [pltpu.VMEM(o.shape, o.dtype) for o in out_shapes]
    call = pl.pallas_call(
        kernel,
        in_specs=[pl.BlockSpec(memory_space=space) for space in in_spaces],
        out_specs=[pl.BlockSpec(memory_space=pltpu.VMEM)] * len(results),
        out_shape=results,
        scratch_shapes=scratch,
        compiler_params=pltpu.CompilerParams(vmem_limit_bytes=limit),
        cost_estimate=cost,
        name=name,
    )

    def apply(*values):
        placed = [
            value if space is pltpu.SMEM else pltpu.with_memory_space_constraint(value, space)
            for value, space in zip(values, in_spaces, strict=True)
        ]
        return call(*placed)

    return apply


def pack_kernel(rows_ref, out_ref):
    row_count = rows_ref.shape[2]
    own = rows_ref.shape[1]
    for k in range(own):
        packed = swap_groups([rows_ref[c, k] for c in range(4)])
        for q in range(4):
            out_ref[pl.ds(q * own * row_count + k, row_count, stride=own), :] = packed[q]


def transform(table_ref, value, turned):
    value_high, value_low = split_high_low(value)
    turned_high, turned_low = split_high_low(turned)
    operand = jnp.concatenate(
        [
            jnp.concatenate([value_high, value_low], axis=1),
            jnp.concatenate([turned_high, turned_low], axis=1),
        ],
        axis=0,
    )
    count = value.shape[0]
    total = jnp.dot(table_ref[...], operand, preferred_element_type=F32)
    total = total[:count] + total[count:]
    return total[:, :LANES] + total[:, LANES:]


def site_kernel(table_ref, rows_ref, out_ref):
    mom_count = rows_ref.shape[0]
    rows = rows_ref[...]
    group = lane_group(rows.shape)
    even = group % 2 == 0
    upper = group >= 2
    sites = transform(table_ref, rows, -times_minus_i(rows)) * (1.0 / mom_count)
    other = pltpu.roll(sites, 2 * GROUP, 1)
    great = sites + other
    less = jnp.where(upper, sites, other)
    great_turn = pltpu.roll(great, GROUP, 1)
    less_turn = pltpu.roll(less, GROUP, 1)
    pair = jnp.where(even, less * great + less_turn * great_turn, less * great_turn - less_turn * great)
    pair_turn = pltpu.roll(pair, GROUP, 1)
    lesser = jnp.where(even, less * pair - less_turn * pair_turn, less * pair_turn + less_turn * pair)
    greater = jnp.where(even, great * pair + great_turn * pair_turn, great * pair_turn - great_turn * pair)
    energy = (-COUPLING * COUPLING) * jnp.where(upper, lesser, greater - lesser)
    out_ref[...] = transform(table_ref, energy, times_minus_i(energy))


PLACES = (2, 1, 3, 0)
FAR = 1


def left_factors(limits_ref, energy_ref, left_ref, split_ref):
    own = left_ref.shape[0]
    block = split_ref.shape[1]
    rows = block // own
    position = limits_ref[0] * LANES + lax.broadcasted_iota(jnp.int32, (block, LANES), 1)
    mask = (position < limits_ref[1]).astype(F32)
    parts = swap_groups([energy_ref[q * block : (q + 1) * block, :] for q in range(4)])
    for c in range(4):
        split_ref[c] = parts[c] * mask
    for k in range(own):
        for pair in range(2):
            real = split_ref[2 * pair, pl.ds(k, rows, stride=own), :]
            imag = split_ref[2 * pair + 1, pl.ds(k, rows, stride=own), :]
            joined = jnp.concatenate(
                [jnp.concatenate([real, -imag], axis=1), jnp.concatenate([imag, real], axis=1)], axis=0
            )
            high, low = split_high_low(joined)
            columns = slice(2 * pair * LANES, 2 * (pair + 1) * LANES)
            left_ref[k, : 2 * rows, columns] = high
            left_ref[k, 2 * rows :, columns] = low


def products_into(left_ref, parts_ref, out_refs, first, prepare=None):
    own = left_ref.shape[0]
    rows = left_ref.shape[1] // 4
    block = own * rows
    columns = slice(first * LANES, (first + len(out_refs)) * LANES)

    def each(k, carry):
        if prepare is not None:
            prepare(k)

        def product(lhs, start, stop):
            both = jnp.dot(lhs, parts_ref[0, k, start:stop, columns], preferred_element_type=F32)
            small = jnp.dot(lhs[: 2 * rows], parts_ref[1, k, start:stop, columns], preferred_element_type=F32)
            return TIME_STEP * (both[: 2 * rows] + both[2 * rows :] + small)

        left = left_ref[k]
        retarded = product(left[:, : 2 * LANES], 0, 2 * LANES)
        lesser = product(left, 2 * LANES, 6 * LANES)
        values = (retarded[:rows], retarded[rows:], lesser[:rows], lesser[rows:])
        for c, value in enumerate(values):
            for n, out_ref in enumerate(out_refs):
                out_ref[pl.ds(c * block + k, rows, stride=own), :] = value[:, n * LANES : (n + 1) * LANES]
        return carry

    lax.fori_loop(0, own // 2, lambda pair, carry: each(2 * pair + 1, each(2 * pair, carry)), 0)


def far_integral_kernel(limits_ref, energy_ref, parts_ref, *refs):
    *out_refs, left_ref, split_ref = refs
    left_factors(limits_ref, energy_ref, left_ref, split_ref)
    products_into(left_ref, parts_ref, out_refs, 0)


def near_integral_kernel(left_ref, parts_ref, *out_refs):
    products_into(left_ref, parts_ref, out_refs, len(PLACES) - len(out_refs))


def first_integral_kernel(limits_ref, energy_ref, stored_ref, *refs):
    *out_refs, parts_ref, left_ref, split_ref, buffer_ref, arrived = refs
    kinds, halves, own, times, _ = stored_ref.shape

    def fetch(k, n):
        source = stored_ref.at[n // halves, n % halves, k]
        return pltpu.make_async_copy(source, buffer_ref.at[k, n], arrived.at[k, n])

    for k in range(own):
        for n in range(kinds * halves):
            fetch(k, n).start()

    left_factors(limits_ref, energy_ref, left_ref, split_ref)

    def prepare(k):
        for n in range(kinds * halves):
            fetch(k, n).wait()
            for m, place in enumerate(PLACES):
                owner = (limits_ref[0] + place) % len(PLACES)
                block = buffer_ref[k, n, :, pl.ds(pl.multiple_of(owner * LANES, LANES), LANES)]
                high, low = split_high_low(block)
                parts_ref[0, k, n * times : (n + 1) * times, m * LANES : (m + 1) * LANES] = high
                parts_ref[1, k, n * times : (n + 1) * times, m * LANES : (m + 1) * LANES] = low

    products_into(left_ref, parts_ref, out_refs, 0, prepare)


def slope_of(parts, state, band_ref):
    block = band_ref.shape[0]
    total = (parts[0][...] + parts[1][...]) + (parts[2][...] + parts[3][...])
    packed = swap_groups([total[c * block : (c + 1) * block] for c in range(4)])
    band = band_ref[...]
    return jnp.concatenate(
        [times_minus_i(band * state[q * block : (q + 1) * block] + packed[q]) for q in range(4)], axis=0
    )


def predict_kernel(first_ref, second_ref, third_ref, own_ref, state_ref, band_ref, out_ref, base_ref):
    state = state_ref[...]
    slope = slope_of((first_ref, second_ref, third_ref, own_ref), state, band_ref)
    out_ref[...] = state + TIME_STEP * slope
    base_ref[...] = state + (0.5 * TIME_STEP) * slope


def correct_kernel(first_ref, second_ref, third_ref, own_ref, state_ref, band_ref, base_ref, out_ref):
    slope = slope_of((first_ref, second_ref, third_ref, own_ref), state_ref[...], band_ref)
    out_ref[...] = base_ref[...] + (0.5 * TIME_STEP) * slope


def last_kernel(first_ref, second_ref, third_ref, own_ref, state_ref, band_ref, base_ref, out_ref, split_ref):
    slope = slope_of((first_ref, second_ref, third_ref, own_ref), state_ref[...], band_ref)
    value = base_ref[...] + (0.5 * TIME_STEP) * slope
    block = band_ref.shape[0]
    parts = swap_groups([value[q * block : (q + 1) * block] for q in range(4)])
    own, rows = out_ref.shape[1], out_ref.shape[2]
    for c in range(4):
        split_ref[c] = parts[c]
        for k in range(own):
            out_ref[c, k] = split_ref[c, pl.ds(k, rows, stride=own), :]


def transform_tables(momentum_map):
    point_x = momentum_map // SIDE
    point_y = momentum_map % SIDE
    winding = (point_x[:, None] * point_x[None, :] + point_y[:, None] * point_y[None, :]) % SIDE
    phases = winding.astype(F32) * (2.0 * jnp.pi / SIDE)
    parts = []
    for table in (jnp.cos(phases), jnp.sin(phases)):
        high = lax.reduce_precision(table, 8, 7)
        parts.append((high.astype(BF16), (table - high).astype(BF16)))
    (cos_high, cos_low), (sin_high, sin_low) = parts
    high = jnp.concatenate([cos_high, sin_high], axis=1)
    return jnp.concatenate([high, jnp.concatenate([cos_low, sin_low], axis=1)], axis=0)


def band_rows(own_map, first_times, offset):
    wave_x = (own_map // SIDE).astype(F32) * (2.0 * jnp.pi / SIDE)
    wave_y = (own_map % SIDE).astype(F32) * (2.0 * jnp.pi / SIDE)
    drift = DRIVE_RATE * ((first_times + offset) * TIME_STEP)
    band = -2.0 * (jnp.cos(wave_x[None, :] + drift[:, None]) + jnp.cos(wave_y[None, :] + drift[:, None]))
    return jnp.broadcast_to(band.reshape(-1, 1), (band.size, LANES))


def body(new_rows, history, momentum_map, step_index, history_len):
    own = new_rows.shape[1]
    row_count = new_rows.shape[2]
    time_count = new_rows.shape[3]
    hist = history.shape[4]
    block = own * row_count
    packed_shape = jax.ShapeDtypeStruct((4 * block, time_count), F32)

    table = transform_tables(momentum_map)
    own_map = lax.dynamic_slice_in_dim(momentum_map, lax.axis_index("mom") * own, own, 0)
    first_times = step_index[0].astype(F32) + jnp.arange(row_count, dtype=jnp.int32).astype(F32)
    bands = [band_rows(own_map, first_times, float(offset)) for offset in range(3)]
    limits = jnp.stack([lax.axis_index("tm"), history_len[0]])

    vmem = pltpu.VMEM
    pack = resident(pack_kernel, [packed_shape], [vmem], "pack")
    stored = 6 * time_count
    parts_shape = jax.ShapeDtypeStruct((2, own, stored, hist), BF16)
    site = resident(site_kernel, [packed_shape], [vmem] * 2, "site")
    tm_size = lax.axis_size("tm")
    split_scratch = vmem((4, block, LANES), F32)
    left_shape = jax.ShapeDtypeStruct((own, 4 * row_count, 4 * LANES), BF16)
    far_integral = resident(
        far_integral_kernel,
        [packed_shape] * FAR + [left_shape],
        [pltpu.SMEM, vmem, vmem],
        "far_integral",
        [split_scratch],
    )
    near = tm_size - FAR
    near_cost = pl.CostEstimate(
        flops=2 * own * 6 * row_count * stored * near * LANES,
        transcendentals=0,
        bytes_accessed=2 * 2 * own * stored * near * LANES,
    )
    near_integral = resident(
        near_integral_kernel, [packed_shape] * near, [vmem, vmem], "near_integral", cost=near_cost
    )
    first_integral = resident(
        first_integral_kernel,
        [packed_shape] * tm_size + [parts_shape],
        [pltpu.SMEM, vmem, pltpu.HBM],
        "first_integral",
        [
            vmem(left_shape.shape, BF16),
            split_scratch,
            vmem((own, 6, time_count, hist), F32),
            pltpu.SemaphoreType.DMA((own, 6)),
        ],
        9 << 20,
    )
    predict = resident(predict_kernel, [packed_shape] * 2, [vmem] * 6, "predict")
    correct = resident(correct_kernel, [packed_shape], [vmem] * 7, "correct")
    last = resident(
        last_kernel, [jax.ShapeDtypeStruct(new_rows.shape, F32)], [vmem] * 7, "last", [split_scratch]
    )
    (state,) = pack(new_rows)

    def turned(value):
        return lax.all_to_all(value, "mom", 0, 0, tiled=True)

    def exchange(partial):
        moved = [
            lax.ppermute(value, "tm", [(t, (t + place) % tm_size) for t in range(tm_size)])
            for value, place in zip(partial[:-1], PLACES[:-1], strict=True)
        ]
        return *moved, partial[-1]

    def energy_of(arrived):
        (energy,) = site(table, arrived)
        return turned(energy)

    first = turned(state)
    first, limits, bands = lax.optimization_barrier((first, limits, bands))
    *partial, stored_parts = first_integral(limits, energy_of(first), history)

    def parts_of(estimate):
        *far, left = far_integral(limits, energy_of(turned(estimate)), stored_parts)
        return exchange(far + list(near_integral(left, stored_parts)))

    for time_step in range(2):
        parts = exchange(partial) if time_step == 0 else parts_of(state)
        estimate, base = predict(*parts, state, bands[time_step])
        (estimate,) = correct(*parts_of(estimate), estimate, bands[time_step + 1], base)
        if time_step == 0:
            (state,) = correct(*parts_of(estimate), estimate, bands[1], base)
    return last(*parts_of(estimate), estimate, bands[2], base)[0]


def solution(mesh):
    return jax.shard_map(
        body,
        mesh=mesh,
        in_specs=(P(None, "mom", None, "tm"), P(None, None, "mom", "tm", None), P(), P(), P()),
        out_specs=P(None, "mom", None, "tm"),
        check_vma=False,
    )
```

```python
import functools

import jax
import jax.numpy as jnp
from jax import lax
from jax.experimental import pallas as pl
from jax.experimental.pallas import tpu as pltpu
from jax.sharding import PartitionSpec as P

SIDE = 16
TIME_STEP = 0.2
COUPLING = 5.0
DRIVE_RATE = 0.3
LANES = 128
GROUP = 32
F32 = jnp.float32
BF16 = jnp.bfloat16


def lane_group(shape):
    return lax.broadcasted_iota(jnp.int32, shape, len(shape) - 1) // GROUP


def swap_groups(blocks):
    group = lane_group(blocks[0].shape)
    outs = []
    for c in range(4):
        out = None
        for q in range(4):
            shift = (GROUP * (q - c)) % LANES
            piece = pltpu.roll(blocks[q], shift, 1) if shift else blocks[q]
            out = piece if out is None else jnp.where(group == q, piece, out)
        outs.append(out)
    return outs


def split_high_low(value):
    high = value.astype(BF16)
    low = (value - high.astype(F32)).astype(BF16)
    return high, low


def times_minus_i(value):
    even = lane_group(value.shape) % 2 == 0
    return jnp.where(even, pltpu.roll(value, LANES - GROUP, 1), -pltpu.roll(value, GROUP, 1))


def resident(kernel, out_shapes, in_spaces, name, scratch=(), limit=4 << 20, cost=None):
    results = [pltpu.VMEM(o.shape, o.dtype) for o in out_shapes]
    call = pl.pallas_call(
        kernel,
        in_specs=[pl.BlockSpec(memory_space=space) for space in in_spaces],
        out_specs=[pl.BlockSpec(memory_space=pltpu.VMEM)] * len(results),
        out_shape=results,
        scratch_shapes=scratch,
        compiler_params=pltpu.CompilerParams(vmem_limit_bytes=limit),
        cost_estimate=cost,
        name=name,
    )

    def apply(*values):
        placed = [
            value if space is pltpu.SMEM else pltpu.with_memory_space_constraint(value, space)
            for value, space in zip(values, in_spaces, strict=True)
        ]
        return call(*placed)

    return apply


def pack_kernel(rows_ref, out_ref, kept_ref):
    row_count = rows_ref.shape[2]
    own = rows_ref.shape[1]
    for k in range(own):
        packed = swap_groups([rows_ref[c, k] for c in range(4)])
        for q in range(4):
            target = pl.ds(q * own * row_count + k, row_count, stride=own)
            out_ref[target, :] = packed[q]
            kept_ref[target, :] = packed[q]


def transform(table_ref, value, turned):
    value_high, value_low = split_high_low(value)
    turned_high, turned_low = split_high_low(turned)
    operand = jnp.concatenate(
        [
            jnp.concatenate([value_high, value_low], axis=1),
            jnp.concatenate([turned_high, turned_low], axis=1),
        ],
        axis=0,
    )
    count = value.shape[0]
    total = jnp.dot(table_ref[...], operand, preferred_element_type=F32)
    total = total[:count] + total[count:]
    return total[:, :LANES] + total[:, LANES:]


def site_kernel(table_ref, rows_ref, out_ref):
    mom_count = rows_ref.shape[0]
    rows = rows_ref[...]
    group = lane_group(rows.shape)
    even = group % 2 == 0
    upper = group >= 2
    sites = transform(table_ref, rows, -times_minus_i(rows)) * (1.0 / mom_count)
    other = pltpu.roll(sites, 2 * GROUP, 1)
    great = sites + other
    less = jnp.where(upper, sites, other)
    great_turn = pltpu.roll(great, GROUP, 1)
    less_turn = pltpu.roll(less, GROUP, 1)
    pair = jnp.where(even, less * great + less_turn * great_turn, less * great_turn - less_turn * great)
    pair_turn = pltpu.roll(pair, GROUP, 1)
    lesser = jnp.where(even, less * pair - less_turn * pair_turn, less * pair_turn + less_turn * pair)
    greater = jnp.where(even, great * pair + great_turn * pair_turn, great * pair_turn - great_turn * pair)
    energy = (-COUPLING * COUPLING) * jnp.where(upper, lesser, greater - lesser)
    out_ref[...] = transform(table_ref, energy, times_minus_i(energy))


PLACES = (2, 1, 3, 0)
FAR = 1


def left_factors(limits_ref, energy_ref, left_ref, split_ref):
    own = left_ref.shape[0]
    block = split_ref.shape[1]
    rows = block // own
    position = limits_ref[0] * LANES + lax.broadcasted_iota(jnp.int32, (block, LANES), 1)
    mask = (position < limits_ref[1]).astype(F32)
    parts = swap_groups([energy_ref[q * block : (q + 1) * block, :] for q in range(4)])
    for c in range(4):
        split_ref[c] = parts[c] * mask
    for k in range(own):
        for pair in range(2):
            real = split_ref[2 * pair, pl.ds(k, rows, stride=own), :]
            imag = split_ref[2 * pair + 1, pl.ds(k, rows, stride=own), :]
            joined = jnp.concatenate(
                [jnp.concatenate([real, -imag], axis=1), jnp.concatenate([imag, real], axis=1)], axis=0
            )
            high, low = split_high_low(joined)
            columns = slice(2 * pair * LANES, 2 * (pair + 1) * LANES)
            left_ref[k, : 2 * rows, columns] = high
            left_ref[k, 2 * rows :, columns] = low


def products_into(left_ref, parts_ref, out_refs, first, together, prepare=None):
    own = left_ref.shape[0]
    rows = left_ref.shape[1] // 4
    block = own * rows
    columns = slice(first * LANES, (first + len(out_refs)) * LANES)

    def each(k, carry):
        if prepare is not None:
            prepare(k)

        def product(lhs, start, stop):
            both = jnp.dot(lhs, parts_ref[0, k, start:stop, columns], preferred_element_type=F32)
            small = jnp.dot(lhs[: 2 * rows], parts_ref[1, k, start:stop, columns], preferred_element_type=F32)
            return TIME_STEP * (both[: 2 * rows] + both[2 * rows :] + small)

        left = left_ref[k]
        retarded = product(left[:, : 2 * LANES], 0, 2 * LANES)
        lesser = product(left, 2 * LANES, 6 * LANES)
        values = (retarded[:rows], retarded[rows:], lesser[:rows], lesser[rows:])
        for c, value in enumerate(values):
            for n, out_ref in enumerate(out_refs):
                out_ref[pl.ds(c * block + k, rows, stride=own), :] = value[:, n * LANES : (n + 1) * LANES]
        return carry

    def several(step, carry):
        for n in range(together):
            carry = each(step * together + n, carry)
        return carry

    if together == own:
        several(0, 0)
    else:
        lax.fori_loop(0, own // together, several, 0)


def far_integral_kernel(limits_ref, energy_ref, parts_ref, *refs):
    *out_refs, left_ref, split_ref = refs
    left_factors(limits_ref, energy_ref, left_ref, split_ref)
    products_into(left_ref, parts_ref, out_refs, 0, 4)


def near_integral_kernel(left_ref, parts_ref, *out_refs):
    products_into(left_ref, parts_ref, out_refs, len(PLACES) - len(out_refs), 1)


def first_integral_kernel(limits_ref, energy_ref, stored_ref, *refs):
    *out_refs, parts_ref, left_ref, split_ref, buffer_ref, arrived = refs
    kinds, halves, own, times, _ = stored_ref.shape

    def fetch(k, n):
        source = stored_ref.at[n // halves, n % halves, k]
        return pltpu.make_async_copy(source, buffer_ref.at[k, n], arrived.at[k, n])

    for k in range(own):
        for n in range(kinds * halves):
            fetch(k, n).start()

    left_factors(limits_ref, energy_ref, left_ref, split_ref)

    def prepare(k):
        for n in range(kinds * halves):
            fetch(k, n).wait()
            for m, place in enumerate(PLACES):
                owner = (limits_ref[0] + place) % len(PLACES)
                block = buffer_ref[k, n, :, pl.ds(pl.multiple_of(owner * LANES, LANES), LANES)]
                high, low = split_high_low(block)
                parts_ref[0, k, n * times : (n + 1) * times, m * LANES : (m + 1) * LANES] = high
                parts_ref[1, k, n * times : (n + 1) * times, m * LANES : (m + 1) * LANES] = low

    products_into(left_ref, parts_ref, out_refs, 0, 1, prepare)


def slope_of(parts, state, band_ref):
    block = band_ref.shape[0]
    total = (parts[0][...] + parts[1][...]) + (parts[2][...] + parts[3][...])
    packed = swap_groups([total[c * block : (c + 1) * block] for c in range(4)])
    band = band_ref[...]
    return jnp.concatenate(
        [times_minus_i(band * state[q * block : (q + 1) * block] + packed[q]) for q in range(4)], axis=0
    )


def predict_kernel(first_ref, second_ref, third_ref, own_ref, state_ref, band_ref, out_ref, base_ref):
    state = state_ref[...]
    slope = slope_of((first_ref, second_ref, third_ref, own_ref), state, band_ref)
    out_ref[...] = state + TIME_STEP * slope
    base_ref[...] = state + (0.5 * TIME_STEP) * slope


def correct_kernel(first_ref, second_ref, third_ref, own_ref, state_ref, band_ref, base_ref, out_ref):
    slope = slope_of((first_ref, second_ref, third_ref, own_ref), state_ref[...], band_ref)
    out_ref[...] = base_ref[...] + (0.5 * TIME_STEP) * slope


def last_kernel(first_ref, second_ref, third_ref, own_ref, state_ref, band_ref, base_ref, out_ref, split_ref):
    slope = slope_of((first_ref, second_ref, third_ref, own_ref), state_ref[...], band_ref)
    value = base_ref[...] + (0.5 * TIME_STEP) * slope
    block = band_ref.shape[0]
    parts = swap_groups([value[q * block : (q + 1) * block] for q in range(4)])
    own, rows = out_ref.shape[1], out_ref.shape[2]
    for c in range(4):
        split_ref[c] = parts[c]
        for k in range(own):
            out_ref[c, k] = split_ref[c, pl.ds(k, rows, stride=own), :]


def transform_tables(momentum_map):
    point_x = momentum_map // SIDE
    point_y = momentum_map % SIDE
    winding = (point_x[:, None] * point_x[None, :] + point_y[:, None] * point_y[None, :]) % SIDE
    phases = winding.astype(F32) * (2.0 * jnp.pi / SIDE)
    parts = []
    for table in (jnp.cos(phases), jnp.sin(phases)):
        high = lax.reduce_precision(table, 8, 7)
        parts.append((high.astype(BF16), (table - high).astype(BF16)))
    (cos_high, cos_low), (sin_high, sin_low) = parts
    high = jnp.concatenate([cos_high, sin_high], axis=1)
    return jnp.concatenate([high, jnp.concatenate([cos_low, sin_low], axis=1)], axis=0)


def band_rows(own_map, first_times, offset):
    wave_x = (own_map // SIDE).astype(F32) * (2.0 * jnp.pi / SIDE)
    wave_y = (own_map % SIDE).astype(F32) * (2.0 * jnp.pi / SIDE)
    drift = DRIVE_RATE * ((first_times + offset) * TIME_STEP)
    band = -2.0 * (jnp.cos(wave_x[None, :] + drift[:, None]) + jnp.cos(wave_y[None, :] + drift[:, None]))
    return jnp.broadcast_to(band.reshape(-1, 1), (band.size, LANES))


def body(new_rows, history, momentum_map, step_index, history_len):
    own = new_rows.shape[1]
    row_count = new_rows.shape[2]
    time_count = new_rows.shape[3]
    hist = history.shape[4]
    block = own * row_count
    packed_shape = jax.ShapeDtypeStruct((4 * block, time_count), F32)

    table = transform_tables(momentum_map)
    own_map = lax.dynamic_slice_in_dim(momentum_map, lax.axis_index("mom") * own, own, 0)
    first_times = step_index[0].astype(F32) + jnp.arange(row_count, dtype=jnp.int32).astype(F32)
    bands = [band_rows(own_map, first_times, float(offset)) for offset in range(3)]
    limits = jnp.stack([lax.axis_index("tm"), history_len[0]])

    vmem = pltpu.VMEM
    pack = resident(pack_kernel, [packed_shape] * 2, [vmem], "pack")
    stored = 6 * time_count
    parts_shape = jax.ShapeDtypeStruct((2, own, stored, hist), BF16)
    site = resident(site_kernel, [packed_shape], [vmem] * 2, "site")
    tm_size = lax.axis_size("tm")
    split_scratch = vmem((4, block, LANES), F32)
    left_shape = jax.ShapeDtypeStruct((own, 4 * row_count, 4 * LANES), BF16)
    far_integral = resident(
        far_integral_kernel,
        [packed_shape] * FAR + [left_shape],
        [pltpu.SMEM, vmem, vmem],
        "far_integral",
        [split_scratch],
    )
    near = tm_size - FAR
    near_cost = pl.CostEstimate(
        flops=2 * own * 6 * row_count * stored * near * LANES,
        transcendentals=0,
        bytes_accessed=2 * 2 * own * stored * near * LANES,
    )
    near_integral = resident(
        near_integral_kernel, [packed_shape] * near, [vmem, vmem], "near_integral", cost=near_cost
    )
    first_integral = resident(
        first_integral_kernel,
        [packed_shape] * tm_size + [parts_shape],
        [pltpu.SMEM, vmem, pltpu.HBM],
        "first_integral",
        [
            vmem(left_shape.shape, BF16),
            split_scratch,
            vmem((own, 6, time_count, hist), F32),
            pltpu.SemaphoreType.DMA((own, 6)),
        ],
        9 << 20,
    )
    predict = resident(predict_kernel, [packed_shape] * 2, [vmem] * 6, "predict")
    correct = resident(correct_kernel, [packed_shape], [vmem] * 7, "correct")
    last = resident(
        last_kernel, [jax.ShapeDtypeStruct(new_rows.shape, F32)], [vmem] * 7, "last", [split_scratch]
    )
    sent, state = pack(new_rows)

    def turned(value):
        return lax.all_to_all(value, "mom", 0, 0, tiled=True)

    def exchange(partial):
        moved = [
            lax.ppermute(value, "tm", [(t, (t + place) % tm_size) for t in range(tm_size)])
            for value, place in zip(partial[:-1], PLACES[:-1], strict=True)
        ]
        return *moved, partial[-1]

    def energy_of(arrived):
        (energy,) = site(table, arrived)
        return turned(energy)

    first = turned(sent)
    first, limits, bands = lax.optimization_barrier((first, limits, bands))
    *partial, stored_parts = first_integral(limits, energy_of(first), history)

    def parts_of(estimate):
        *far, left = far_integral(limits, energy_of(turned(estimate)), stored_parts)
        return exchange(far + list(near_integral(left, stored_parts)))

    for time_step in range(2):
        parts = exchange(partial) if time_step == 0 else parts_of(state)
        estimate, base = predict(*parts, state, bands[time_step])
        (estimate,) = correct(*parts_of(estimate), estimate, bands[time_step + 1], base)
        if time_step == 0:
            (state,) = correct(*parts_of(estimate), estimate, bands[1], base)
    return last(*parts_of(estimate), estimate, bands[2], base)[0]


def solution(mesh):
    return jax.shard_map(
        body,
        mesh=mesh,
        in_specs=(P(None, "mom", None, "tm"), P(None, None, "mom", "tm", None), P(), P(), P()),
        out_specs=P(None, "mom", None, "tm"),
        check_vma=False,
    )
```

```python
import functools

import jax
import jax.numpy as jnp
from jax import lax
from jax.experimental import pallas as pl
from jax.experimental.pallas import tpu as pltpu
from jax.sharding import PartitionSpec as P

SIDE = 16
TIME_STEP = 0.2
COUPLING = 5.0
DRIVE_RATE = 0.3
LANES = 128
GROUP = 32
F32 = jnp.float32
BF16 = jnp.bfloat16


def lane_group(shape):
    return lax.broadcasted_iota(jnp.int32, shape, len(shape) - 1) // GROUP


def swap_groups(blocks):
    group = lane_group(blocks[0].shape)
    outs = []
    for c in range(4):
        out = None
        for q in range(4):
            shift = (GROUP * (q - c)) % LANES
            piece = pltpu.roll(blocks[q], shift, 1) if shift else blocks[q]
            out = piece if out is None else jnp.where(group == q, piece, out)
        outs.append(out)
    return outs


def split_high_low(value):
    high = value.astype(BF16)
    low = (value - high.astype(F32)).astype(BF16)
    return high, low


def times_minus_i(value):
    even = lane_group(value.shape) % 2 == 0
    return jnp.where(even, pltpu.roll(value, LANES - GROUP, 1), -pltpu.roll(value, GROUP, 1))


def resident(kernel, out_shapes, in_spaces, name, scratch=(), limit=4 << 20, cost=None):
    results = [pltpu.VMEM(o.shape, o.dtype) for o in out_shapes]
    call = pl.pallas_call(
        kernel,
        in_specs=[pl.BlockSpec(memory_space=space) for space in in_spaces],
        out_specs=[pl.BlockSpec(memory_space=pltpu.VMEM)] * len(results),
        out_shape=results,
        scratch_shapes=scratch,
        compiler_params=pltpu.CompilerParams(vmem_limit_bytes=limit),
        cost_estimate=cost,
        name=name,
    )

    def apply(*values):
        placed = [
            value if space is pltpu.SMEM else pltpu.with_memory_space_constraint(value, space)
            for value, space in zip(values, in_spaces, strict=True)
        ]
        return call(*placed)

    return apply


def pack_kernel(rows_ref, out_ref, kept_ref, buffer_ref, arrived):
    row_count = rows_ref.shape[2]
    own = rows_ref.shape[1]
    copies = [pltpu.make_async_copy(rows_ref.at[:, k], buffer_ref.at[k], arrived.at[k]) for k in range(own)]
    for copy in copies:
        copy.start()
    for k in range(own):
        copies[k].wait()
        packed = swap_groups([buffer_ref[k, c] for c in range(4)])
        for q in range(4):
            target = pl.ds(q * own * row_count + k, row_count, stride=own)
            out_ref[target, :] = packed[q]
            kept_ref[target, :] = packed[q]


def transform(table_ref, value, turned):
    value_high, value_low = split_high_low(value)
    turned_high, turned_low = split_high_low(turned)
    operand = jnp.concatenate(
        [
            jnp.concatenate([value_high, value_low], axis=1),
            jnp.concatenate([turned_high, turned_low], axis=1),
        ],
        axis=0,
    )
    count = value.shape[0]
    total = jnp.dot(table_ref[...], operand, preferred_element_type=F32)
    total = total[:count] + total[count:]
    return total[:, :LANES] + total[:, LANES:]


def site_kernel(table_ref, rows_ref, out_ref):
    mom_count = rows_ref.shape[0]
    rows = rows_ref[...]
    group = lane_group(rows.shape)
    even = group % 2 == 0
    upper = group >= 2
    sites = transform(table_ref, rows, -times_minus_i(rows)) * (1.0 / mom_count)
    other = pltpu.roll(sites, 2 * GROUP, 1)
    great = sites + other
    less = jnp.where(upper, sites, other)
    great_turn = pltpu.roll(great, GROUP, 1)
    less_turn = pltpu.roll(less, GROUP, 1)
    pair = jnp.where(even, less * great + less_turn * great_turn, less * great_turn - less_turn * great)
    pair_turn = pltpu.roll(pair, GROUP, 1)
    lesser = jnp.where(even, less * pair - less_turn * pair_turn, less * pair_turn + less_turn * pair)
    greater = jnp.where(even, great * pair + great_turn * pair_turn, great * pair_turn - great_turn * pair)
    energy = (-COUPLING * COUPLING) * jnp.where(upper, lesser, greater - lesser)
    out_ref[...] = transform(table_ref, energy, times_minus_i(energy))


PLACES = (2, 1, 3, 0)
FAR = 1


def left_factors(limits_ref, energy_ref, left_ref, split_ref):
    own = left_ref.shape[0]
    block = split_ref.shape[1]
    rows = block // own
    position = limits_ref[0] * LANES + lax.broadcasted_iota(jnp.int32, (block, LANES), 1)
    mask = (position < limits_ref[1]).astype(F32)
    parts = swap_groups([energy_ref[q * block : (q + 1) * block, :] for q in range(4)])
    for c in range(4):
        split_ref[c] = parts[c] * mask
    for k in range(own):
        for pair in range(2):
            real = split_ref[2 * pair, pl.ds(k, rows, stride=own), :]
            imag = split_ref[2 * pair + 1, pl.ds(k, rows, stride=own), :]
            joined = jnp.concatenate(
                [jnp.concatenate([real, -imag], axis=1), jnp.concatenate([imag, real], axis=1)], axis=0
            )
            high, low = split_high_low(joined)
            columns = slice(2 * pair * LANES, 2 * (pair + 1) * LANES)
            left_ref[k, : 2 * rows, columns] = high
            left_ref[k, 2 * rows :, columns] = low


def products_into(left_ref, parts_ref, out_refs, first, together, prepare=None):
    own = left_ref.shape[0]
    rows = left_ref.shape[1] // 4
    block = own * rows
    columns = slice(first * LANES, (first + len(out_refs)) * LANES)

    def each(k, carry):
        if prepare is not None:
            prepare(k)

        def product(lhs, start, stop):
            both = jnp.dot(lhs, parts_ref[0, k, start:stop, columns], preferred_element_type=F32)
            small = jnp.dot(lhs[: 2 * rows], parts_ref[1, k, start:stop, columns], preferred_element_type=F32)
            return TIME_STEP * (both[: 2 * rows] + both[2 * rows :] + small)

        left = left_ref[k]
        retarded = product(left[:, : 2 * LANES], 0, 2 * LANES)
        lesser = product(left, 2 * LANES, 6 * LANES)
        values = (retarded[:rows], retarded[rows:], lesser[:rows], lesser[rows:])
        for c, value in enumerate(values):
            for n, out_ref in enumerate(out_refs):
                out_ref[pl.ds(c * block + k, rows, stride=own), :] = value[:, n * LANES : (n + 1) * LANES]
        return carry

    def several(step, carry):
        for n in range(together):
            carry = each(step * together + n, carry)
        return carry

    if together == own:
        several(0, 0)
    else:
        lax.fori_loop(0, own // together, several, 0)


def far_integral_kernel(limits_ref, energy_ref, parts_ref, *refs):
    *out_refs, left_ref, split_ref = refs
    left_factors(limits_ref, energy_ref, left_ref, split_ref)
    products_into(left_ref, parts_ref, out_refs, 0, 4)


def near_integral_kernel(left_ref, parts_ref, *out_refs):
    products_into(left_ref, parts_ref, out_refs, len(PLACES) - len(out_refs), 1)


def first_integral_kernel(limits_ref, energy_ref, stored_ref, *refs):
    *out_refs, parts_ref, left_ref, split_ref, buffer_ref, arrived = refs
    kinds, halves, own, times, _ = stored_ref.shape

    def fetch(k, n):
        source = stored_ref.at[n // halves, n % halves, k]
        return pltpu.make_async_copy(source, buffer_ref.at[k, n], arrived.at[k, n])

    for k in range(own):
        for n in range(kinds * halves):
            fetch(k, n).start()

    left_factors(limits_ref, energy_ref, left_ref, split_ref)

    def prepare(k):
        for n in range(kinds * halves):
            fetch(k, n).wait()
            for m, place in enumerate(PLACES):
                owner = (limits_ref[0] + place) % len(PLACES)
                block = buffer_ref[k, n, :, pl.ds(pl.multiple_of(owner * LANES, LANES), LANES)]
                high, low = split_high_low(block)
                parts_ref[0, k, n * times : (n + 1) * times, m * LANES : (m + 1) * LANES] = high
                parts_ref[1, k, n * times : (n + 1) * times, m * LANES : (m + 1) * LANES] = low

    products_into(left_ref, parts_ref, out_refs, 0, 2, prepare)


def slope_of(parts, state, band_ref):
    block = band_ref.shape[0]
    total = (parts[0][...] + parts[1][...]) + (parts[2][...] + parts[3][...])
    packed = swap_groups([total[c * block : (c + 1) * block] for c in range(4)])
    band = band_ref[...]
    return jnp.concatenate(
        [times_minus_i(band * state[q * block : (q + 1) * block] + packed[q]) for q in range(4)], axis=0
    )


def predict_kernel(first_ref, second_ref, third_ref, own_ref, state_ref, band_ref, out_ref, base_ref):
    state = state_ref[...]
    slope = slope_of((first_ref, second_ref, third_ref, own_ref), state, band_ref)
    out_ref[...] = state + TIME_STEP * slope
    base_ref[...] = state + (0.5 * TIME_STEP) * slope


def correct_kernel(first_ref, second_ref, third_ref, own_ref, state_ref, band_ref, base_ref, out_ref):
    slope = slope_of((first_ref, second_ref, third_ref, own_ref), state_ref[...], band_ref)
    out_ref[...] = base_ref[...] + (0.5 * TIME_STEP) * slope


def last_kernel(first_ref, second_ref, third_ref, own_ref, state_ref, band_ref, base_ref, out_ref, split_ref):
    slope = slope_of((first_ref, second_ref, third_ref, own_ref), state_ref[...], band_ref)
    value = base_ref[...] + (0.5 * TIME_STEP) * slope
    block = band_ref.shape[0]
    parts = swap_groups([value[q * block : (q + 1) * block] for q in range(4)])
    own, rows = out_ref.shape[1], out_ref.shape[2]
    for c in range(4):
        split_ref[c] = parts[c]
        for k in range(own):
            out_ref[c, k] = split_ref[c, pl.ds(k, rows, stride=own), :]


def transform_tables(momentum_map):
    point_x = momentum_map // SIDE
    point_y = momentum_map % SIDE
    winding = (point_x[:, None] * point_x[None, :] + point_y[:, None] * point_y[None, :]) % SIDE
    phases = winding.astype(F32) * (2.0 * jnp.pi / SIDE)
    parts = []
    for table in (jnp.cos(phases), jnp.sin(phases)):
        high = lax.reduce_precision(table, 8, 7)
        parts.append((high.astype(BF16), (table - high).astype(BF16)))
    (cos_high, cos_low), (sin_high, sin_low) = parts
    high = jnp.concatenate([cos_high, sin_high], axis=1)
    return jnp.concatenate([high, jnp.concatenate([cos_low, sin_low], axis=1)], axis=0)


def band_rows(own_map, first_times, offset):
    wave_x = (own_map // SIDE).astype(F32) * (2.0 * jnp.pi / SIDE)
    wave_y = (own_map % SIDE).astype(F32) * (2.0 * jnp.pi / SIDE)
    drift = DRIVE_RATE * ((first_times + offset) * TIME_STEP)
    band = -2.0 * (jnp.cos(wave_x[None, :] + drift[:, None]) + jnp.cos(wave_y[None, :] + drift[:, None]))
    return jnp.broadcast_to(band.reshape(-1, 1), (band.size, LANES))


def body(new_rows, history, momentum_map, step_index, history_len):
    own = new_rows.shape[1]
    row_count = new_rows.shape[2]
    time_count = new_rows.shape[3]
    hist = history.shape[4]
    block = own * row_count
    packed_shape = jax.ShapeDtypeStruct((4 * block, time_count), F32)

    table = transform_tables(momentum_map)
    own_map = lax.dynamic_slice_in_dim(momentum_map, lax.axis_index("mom") * own, own, 0)
    first_times = step_index[0].astype(F32) + jnp.arange(row_count, dtype=jnp.int32).astype(F32)
    bands = [band_rows(own_map, first_times, float(offset)) for offset in range(3)]
    limits = jnp.stack([lax.axis_index("tm"), history_len[0]])

    vmem = pltpu.VMEM
    pack = resident(
        pack_kernel,
        [packed_shape] * 2,
        [pltpu.HBM],
        "pack",
        [vmem((own, 4, row_count, time_count), F32), pltpu.SemaphoreType.DMA((own,))],
    )
    stored = 6 * time_count
    parts_shape = jax.ShapeDtypeStruct((2, own, stored, hist), BF16)
    site = resident(site_kernel, [packed_shape], [vmem] * 2, "site")
    tm_size = lax.axis_size("tm")
    split_scratch = vmem((4, block, LANES), F32)
    left_shape = jax.ShapeDtypeStruct((own, 4 * row_count, 4 * LANES), BF16)
    far_integral = resident(
        far_integral_kernel,
        [packed_shape] * FAR + [left_shape],
        [pltpu.SMEM, vmem, vmem],
        "far_integral",
        [split_scratch],
    )
    near = tm_size - FAR
    near_cost = pl.CostEstimate(
        flops=2 * own * 6 * row_count * stored * near * LANES,
        transcendentals=0,
        bytes_accessed=2 * 2 * own * stored * near * LANES,
    )
    near_integral = resident(
        near_integral_kernel, [packed_shape] * near, [vmem, vmem], "near_integral", cost=near_cost
    )
    first_integral = resident(
        first_integral_kernel,
        [packed_shape] * tm_size + [parts_shape],
        [pltpu.SMEM, vmem, pltpu.HBM],
        "first_integral",
        [
            vmem(left_shape.shape, BF16),
            split_scratch,
            vmem((own, 6, time_count, hist), F32),
            pltpu.SemaphoreType.DMA((own, 6)),
        ],
        9 << 20,
    )
    predict = resident(predict_kernel, [packed_shape] * 2, [vmem] * 6, "predict")
    correct = resident(correct_kernel, [packed_shape], [vmem] * 7, "correct")
    last = resident(
        last_kernel, [jax.ShapeDtypeStruct(new_rows.shape, F32)], [vmem] * 7, "last", [split_scratch]
    )
    sent, state = pack(new_rows)

    def turned(value):
        return lax.all_to_all(value, "mom", 0, 0, tiled=True)

    def exchange(partial):
        moved = [
            lax.ppermute(value, "tm", [(t, (t + place) % tm_size) for t in range(tm_size)])
            for value, place in zip(partial[:-1], PLACES[:-1], strict=True)
        ]
        return *moved, partial[-1]

    def energy_of(arrived):
        (energy,) = site(table, arrived)
        return turned(energy)

    first = turned(sent)
    first, limits, bands = lax.optimization_barrier((first, limits, bands))
    *partial, stored_parts = first_integral(limits, energy_of(first), history)

    def parts_of(estimate):
        *far, left = far_integral(limits, energy_of(turned(estimate)), stored_parts)
        return exchange(far + list(near_integral(left, stored_parts)))

    for time_step in range(2):
        parts = exchange(partial) if time_step == 0 else parts_of(state)
        estimate, base = predict(*parts, state, bands[time_step])
        (estimate,) = correct(*parts_of(estimate), estimate, bands[time_step + 1], base)
        if time_step == 0:
            (state,) = correct(*parts_of(estimate), estimate, bands[1], base)
    return last(*parts_of(estimate), estimate, bands[2], base)[0]


def solution(mesh):
    return jax.shard_map(
        body,
        mesh=mesh,
        in_specs=(P(None, "mom", None, "tm"), P(None, None, "mom", "tm", None), P(), P(), P()),
        out_specs=P(None, "mom", None, "tm"),
        check_vma=False,
    )
```
